32 devices in a mesh: dp: 8 (over z, y), expert: 4 (over x, core).
Axes of the slice: x: 2, y: 2, z: 4, core: 2. Of those that a mesh axis runs over, the one named last changes fastest.
Arguments:
- expert_ids: int32 [4096, 2], P(('dp', 'expert')), parts along dimension 0, may hold values from 0 to 1, as said below
- gate_weights: float32 [4096, 2], P(('dp', 'expert')), parts along dimension 0, may hold values from 0.2 to 1
- hidden: bfloat16 [4096, 2, 1024], P(('dp', 'expert')), parts along dimension 0, may hold values from -6 to 6
- hot_down: bfloat16 [1024, 3584], P(None, 'expert'), may hold values from -0.1875 to 0.1875
- cold_down: bfloat16 [1024, 3584], P(None, 'expert'), may hold values from -0.1875 to 0.1875
Outputs:
- mixed: bfloat16 [4096, 3584], P(('dp', 'expert')), parts along dimension 0
The draws below stay inside these ranges and needn't reach their ends.
There are 8 independent parts, one for each index of `dp`. The reference program is written for one: setup_inputs(seed, part) draws one part's arguments, and reference() takes and returns one part's arrays. A program takes and returns all parts, laid end to end along the dimension named above; an argument that names none is the same for every part. Nothing has to cross between parts.
Inputs may be any that keep to these rules, and one draw needn't show every extreme that they name: `expert_ids`: each token names 2 different experts. Among the 128 tokens of one device (aligned blocks) expert 1 is named by exactly 128 tokens and no expert by more than 128; one rarely chosen expert, the same for every device, is named by exactly 128 tokens of each device.
All inputs are finite; a program needn't handle non-finite values.
Results may differ from the reference program's by a relative error of at most 0.0042.
Values may be sent and summed in bfloat16 or wider, within the bound.
No kernel may reach another device: no remote copies, remote signals or barrier semaphores. Data moves between devices by JAX's collectives and lax.ppermute only.
A program may use at most 64 MiB of HBM per device.

```python
import jax
import jax.numpy as jnp
from jax import lax

D = 3584
FF = 1024
TOPK = 2
TOK_DEV = 128
COLD = 1
CAP = 128
TOKENS = 512
N_EXPERT = 4


def draw_expert_ids(key, part):
    key_perm = jax.random.fold_in(key, 11)
    key_heavy = jax.random.fold_in(key, 12)
    key_step = jax.random.fold_in(key, 13)
    key_swap = jax.random.fold_in(key, 14)
    block_keys = jax.random.split(key_perm, N_EXPERT)
    ranks = jax.vmap(lambda k: jax.random.permutation(k, TOK_DEV))(block_keys).reshape(TOKENS).astype(jnp.int32)
    heavy = jax.random.randint(key_heavy, (), 0, COLD).astype(jnp.int32)
    steps = jax.random.randint(key_step, (TOKENS,), 0, max(COLD - 1, 1)).astype(jnp.int32)
    other_cold = ((heavy + 1 + steps) % COLD).astype(jnp.int32)
    names_heavy = ranks >= TOK_DEV - CAP
    is_hot = ranks < CAP
    first = jnp.where(names_heavy, jnp.full((TOKENS,), 0, jnp.int32) + heavy, other_cold).astype(jnp.int32)
    second = jnp.where(is_hot, jnp.full((TOKENS,), COLD, jnp.int32), other_cold).astype(jnp.int32)
    swap = jax.random.randint(key_swap, (TOKENS,), 0, 2).astype(jnp.int32) == 1
    left = jnp.where(swap, second, first)
    right = jnp.where(swap, first, second)
    return jnp.stack([left, right], axis=1).astype(jnp.int32)


def shard_levels(rng, shape, pieces, low, largest):
    factor_of = 1.0
    for dim, parts in pieces:
        steps = jax.random.uniform(jax.random.fold_in(jax.random.fold_in(rng, 6), dim), (parts,), jnp.float32, low / len(pieces), largest / len(pieces))
        factor_of = factor_of * jnp.repeat(jnp.exp(steps), shape[dim] // parts).reshape((-1,) + (1,) * (len(shape) - 1 - dim))
    return factor_of


def bell_draw(key, shape, scale, bound, shards=(), kind=jnp.bfloat16):
    result = jax.random.normal(key, shape, jnp.float32) * scale
    if len(shards) > 0:
        result = shard_levels(key, shape, shards, -0.22, 0.18) * result
    return jnp.clip(result, min=-bound, max=bound).astype(kind)


def setup_inputs(seed: int = 0, part: int = 0) -> dict:
    keys = jax.random.split(jax.random.key(seed), 6)
    part_splits = jax.random.split(jax.random.fold_in(keys[5], part), 6)
    return {
        "expert_ids": draw_expert_ids(jax.random.fold_in(jax.random.fold_in(keys[5], part), 71), part),
        "gate_weights": jnp.clip(0.2 + 0.8 * jax.random.uniform(part_splits[1], (TOKENS, TOPK), jnp.float32) ** shard_levels(part_splits[1], (TOKENS, TOPK), ((0, 4),), -0.2, 0.2), 0.2, 1.0),
        "hidden": bell_draw(part_splits[2], (TOKENS, TOPK, FF), 1.0, 6.0, ((0, 4),)),
        "hot_down": bell_draw(keys[3], (FF, D), FF ** -0.5, 0.1875, ((1, 4),)),
        "cold_down": bell_draw(keys[4], (FF, COLD * D), FF ** -0.5, 0.1875, ((1, 4),)),
    }


def reference(expert_ids, gate_weights, hidden, hot_down, cold_down):
    rows_all = TOKENS * TOPK
    slots_all = N_EXPERT * CAP
    flat_hidden = hidden.reshape(rows_all, FF)
    flat_ids = expert_ids.reshape(rows_all)
    flat_gates = gate_weights.reshape(rows_all)
    summed = jnp.zeros((rows_all, D), jnp.float32)
    for expert in range(COLD):
        matches = flat_ids == expert
        found = jnp.sum(matches.astype(jnp.int32)).astype(jnp.int32)
        picked = jnp.nonzero(matches, size=slots_all, fill_value=0)[0].astype(jnp.int32)
        is_real = jnp.arange(slots_all, dtype=jnp.int32) < found
        chosen_rows = flat_hidden[picked]
        weight_block = cold_down[:, expert * D:(expert + 1) * D]
        outputs = jnp.dot(chosen_rows, weight_block, preferred_element_type=jnp.float32).astype(jnp.bfloat16)
        outputs = lax.optimization_barrier(outputs).astype(jnp.float32)
        scale_rows = jnp.where(is_real, flat_gates[picked], jnp.zeros((), flat_gates.dtype))
        summed = summed.at[picked].add(outputs * scale_rows[:, None])
    hot_chosen = expert_ids == COLD
    hot_rows = jnp.sum(jnp.where(hot_chosen[:, :, None], hidden, jnp.zeros((), hidden.dtype)), axis=1).astype(hidden.dtype)
    hot_gate = jnp.sum(jnp.where(hot_chosen, gate_weights, jnp.zeros((), gate_weights.dtype)), axis=1)
    hot_out = jnp.dot(hot_rows, hot_down, preferred_element_type=jnp.float32)
    mixed = summed.reshape(TOKENS, TOPK, D).sum(axis=1) + hot_gate[:, None] * hot_out
    return mixed.astype(jnp.bfloat16)
```

```python
import jax
import jax.numpy as jnp
from jax import lax
from jax.sharding import PartitionSpec as P


def general_body(expert_ids, gate_weights, hidden, hot_down, cold_down):
    devices = lax.axis_size("expert")
    group_size = min(4, devices)
    cold_count = devices // group_size
    experts_all = cold_count + 1
    tok_rows, top_count, hidden_width = hidden.shape
    capacity = 3 * tok_rows // 4 + tok_rows // 4 * (3 - min(experts_all, 3))
    flat_rows = tok_rows * top_count
    flat_hidden = hidden.reshape(flat_rows, hidden_width)
    flat_ids = expert_ids.reshape(flat_rows)
    hot_chosen = expert_ids == cold_count
    hot_rows = jnp.sum(
        jnp.where(hot_chosen[:, :, None], hidden, jnp.zeros((), hidden.dtype)), axis=1
    )
    hot_gate = jnp.sum(jnp.where(hot_chosen, gate_weights, jnp.zeros((), jnp.float32)), axis=1)
    hot_out = jnp.dot(
        hot_rows,
        lax.all_gather(hot_down, "expert", axis=1, tiled=True),
        preferred_element_type=jnp.float32,
    )
    hot_term = hot_gate[:, None] * hot_out
    onehot_expert = (flat_ids[None, :] == jnp.arange(cold_count, dtype=jnp.int32)[:, None]).astype(
        jnp.int32
    )
    slot_ranks = jnp.sum(onehot_expert * (jnp.cumsum(onehot_expert, axis=1) - 1), axis=0)
    slot_index = jnp.where(flat_ids < cold_count, flat_ids * capacity + slot_ranks, -1)
    placing = (
        jnp.arange(cold_count * capacity, dtype=jnp.int32)[:, None] == slot_index[None, :]
    ).astype(jnp.bfloat16)
    send_rows = jnp.dot(placing, flat_hidden, preferred_element_type=jnp.float32).astype(
        jnp.bfloat16
    )
    copies = jnp.broadcast_to(
        send_rows.reshape(cold_count, 1, capacity, hidden_width),
        (cold_count, group_size, capacity, hidden_width),
    ).reshape(devices, capacity, hidden_width)
    outputs = jnp.einsum(
        "nsf,fd->nsd",
        lax.all_to_all(copies, "expert", split_axis=0, concat_axis=0, tiled=True),
        cold_down,
        preferred_element_type=jnp.float32,
    ).astype(jnp.bfloat16)
    returned = lax.all_to_all(outputs, "expert", split_axis=0, concat_axis=0, tiled=True)
    column_blocks = returned.reshape(cold_count, group_size, capacity, -1)
    placing_blocks = placing.reshape(cold_count, capacity, flat_rows)
    row_outputs = jnp.einsum(
        "ecr,egcd->rgd", placing_blocks, column_blocks, preferred_element_type=jnp.float32
    )
    row_outputs = row_outputs.reshape(tok_rows, top_count, -1)
    scaled = row_outputs * gate_weights[:, :, None]
    cold_term = jnp.sum(scaled, axis=1)
    return (cold_term + hot_term).astype(jnp.bfloat16)


def scaled_rows(expert_ids, gate_weights, hidden):
    parts = []
    for expert in range(2):
        gates = jnp.where(expert_ids == expert, gate_weights, jnp.zeros((), jnp.float32))
        rows = jnp.sum(gates[:, :, None] * hidden.astype(jnp.float32), axis=1)
        parts.append(rows.astype(hidden.dtype))
    return parts


def project(rows, weights):
    total = jnp.dot(rows[0], weights[0], preferred_element_type=jnp.float32)
    total += jnp.dot(rows[1], weights[1], preferred_element_type=jnp.float32)
    return total.astype(rows[0].dtype)


def pair_body(expert_ids, gate_weights, hidden, hot_down, cold_down):
    devices = lax.axis_size("expert")
    near = [(i, i ^ 1) for i in range(devices)]
    far = [(i, i ^ 2) for i in range(devices)]
    me = lax.axis_index("expert")
    tok_rows = hidden.shape[0]
    columns = hot_down.shape[1]
    cuts = [0, tok_rows // 2, tok_rows]
    rows = [
        scaled_rows(expert_ids[a:b], gate_weights[a:b], hidden[a:b])
        for a, b in zip(cuts[:-1], cuts[1:])
    ]
    moved = [
        lax.ppermute(jnp.concatenate(r, axis=1), "expert", far) for r in rows
    ]
    own = (cold_down, hot_down)
    partner = (lax.ppermute(cold_down, "expert", near), lax.ppermute(hot_down, "expert", near))
    width = hidden.shape[2]
    out = jnp.zeros((tok_rows, columns * devices), hidden.dtype)
    mine_at, near_at = me * columns, (me ^ 1) * columns
    far_mine_at, far_near_at = (me ^ 2) * columns, (me ^ 3) * columns
    back = []
    for m in moved:
        both = (m[:, :width], m[:, width:])
        result = jnp.concatenate([project(both, own), project(both, partner)], axis=1)
        back.append(lax.ppermute(result, "expert", far))
    whole = [jnp.concatenate(p, axis=0) for p in zip(*rows)]
    out = lax.dynamic_update_slice(out, project(whole, own), (0, mine_at))
    out = lax.dynamic_update_slice(out, project(whole, partner), (0, near_at))
    for b, a in zip(back, cuts[:-1]):
        out = lax.dynamic_update_slice(out, b[:, :columns], (a, far_mine_at))
        out = lax.dynamic_update_slice(out, b[:, columns:], (a, far_near_at))
    return out


def solution(mesh):
    devices = mesh.shape["expert"]
    body = pair_body if devices == 4 else general_body
    return jax.shard_map(
        body,
        mesh=mesh,
        in_specs=(
            P(("dp", "expert"), None),
            P(("dp", "expert"), None),
            P(("dp", "expert"), None, None),
            P(None, "expert"),
            P(None, "expert"),
        ),
        out_specs=P(("dp", "expert"), None),
        check_vma=False,
    )
```

```python
import functools

import jax
import jax.numpy as jnp
from jax import lax
from jax.experimental import pallas as pl
from jax.experimental.pallas import tpu as pltpu
from jax.sharding import PartitionSpec as P

VMEM = pl.BlockSpec(memory_space=pltpu.VMEM)
ANY = pl.BlockSpec(memory_space=pl.ANY)
SLAB = 128
CUTS = (0, 5, 11, 16)


def general_body(expert_ids, gate_weights, hidden, hot_down, cold_down):
    devices = lax.axis_size("expert")
    group_size = min(4, devices)
    cold_count = devices // group_size
    experts_all = cold_count + 1
    tok_rows, top_count, hidden_width = hidden.shape
    capacity = 3 * tok_rows // 4 + tok_rows // 4 * (3 - min(experts_all, 3))
    flat_rows = tok_rows * top_count
    flat_hidden = hidden.reshape(flat_rows, hidden_width)
    flat_ids = expert_ids.reshape(flat_rows)
    hot_chosen = expert_ids == cold_count
    hot_rows = jnp.sum(
        jnp.where(hot_chosen[:, :, None], hidden, jnp.zeros((), hidden.dtype)), axis=1
    )
    hot_gate = jnp.sum(jnp.where(hot_chosen, gate_weights, jnp.zeros((), jnp.float32)), axis=1)
    hot_out = jnp.dot(
        hot_rows,
        lax.all_gather(hot_down, "expert", axis=1, tiled=True),
        preferred_element_type=jnp.float32,
    )
    hot_term = hot_gate[:, None] * hot_out
    onehot_expert = (flat_ids[None, :] == jnp.arange(cold_count, dtype=jnp.int32)[:, None]).astype(
        jnp.int32
    )
    slot_ranks = jnp.sum(onehot_expert * (jnp.cumsum(onehot_expert, axis=1) - 1), axis=0)
    slot_index = jnp.where(flat_ids < cold_count, flat_ids * capacity + slot_ranks, -1)
    placing = (
        jnp.arange(cold_count * capacity, dtype=jnp.int32)[:, None] == slot_index[None, :]
    ).astype(jnp.bfloat16)
    send_rows = jnp.dot(placing, flat_hidden, preferred_element_type=jnp.float32).astype(
        jnp.bfloat16
    )
    copies = jnp.broadcast_to(
        send_rows.reshape(cold_count, 1, capacity, hidden_width),
        (cold_count, group_size, capacity, hidden_width),
    ).reshape(devices, capacity, hidden_width)
    outputs = jnp.einsum(
        "nsf,fd->nsd",
        lax.all_to_all(copies, "expert", split_axis=0, concat_axis=0, tiled=True),
        cold_down,
        preferred_element_type=jnp.float32,
    ).astype(jnp.bfloat16)
    returned = lax.all_to_all(outputs, "expert", split_axis=0, concat_axis=0, tiled=True)
    column_blocks = returned.reshape(cold_count, group_size, capacity, -1)
    placing_blocks = placing.reshape(cold_count, capacity, flat_rows)
    row_outputs = jnp.einsum(
        "ecr,egcd->rgd", placing_blocks, column_blocks, preferred_element_type=jnp.float32
    )
    row_outputs = row_outputs.reshape(tok_rows, top_count, -1)
    scaled = row_outputs * gate_weights[:, :, None]
    cold_term = jnp.sum(scaled, axis=1)
    return (cold_term + hot_term).astype(jnp.bfloat16)


def near_core(*arrays):
    return [pltpu.with_memory_space_constraint(a, pltpu.VMEM) for a in arrays]


def in_hbm(*arrays):
    return [pltpu.with_memory_space_constraint(a, pltpu.HBM) for a in arrays]


def limit(mib):
    return pltpu.CompilerParams(vmem_limit_bytes=mib << 20)


def rows_of(hidden_ref, start, rows_ref, sem):
    flat = hidden_ref.reshape(hidden_ref.shape[0] * hidden_ref.shape[1], hidden_ref.shape[2])
    return pltpu.make_async_copy(flat.at[pl.ds(start, rows_ref.shape[0])], rows_ref, sem)


def take_kernel(start, hidden_ref, rows_ref, sems):
    copy = rows_of(hidden_ref, start, rows_ref, sems.at[0])
    copy.start()
    copy.wait()


def first_take_kernel(start, hidden_ref, ids_ref, weights_ref, rows_ref, gates_ref, ids, weights, sems):
    copies = [
        rows_of(hidden_ref, start, rows_ref, sems.at[0]),
        pltpu.make_async_copy(ids_ref, ids, sems.at[1]),
        pltpu.make_async_copy(weights_ref, weights, sems.at[2]),
    ]
    for copy in copies:
        copy.start()
    for copy in copies[1:]:
        copy.wait()
    for e in range(2):
        gates_ref[2 * e : 2 * e + 2, :] = jnp.where(ids[...] == e, weights[...], 0.0)
    copies[0].wait()


def take(hidden, start, tokens, choice=()):
    _, choices, depth = hidden.shape
    shapes = [pltpu.VMEM((tokens * choices, depth), hidden.dtype)]
    scratch = [pltpu.SemaphoreType.DMA((3,))]
    if choice:
        shapes.append(pltpu.VMEM((2 * choices, hidden.shape[0]), choice[1].dtype))
        scratch = [pltpu.VMEM(c.shape, c.dtype) for c in choice] + scratch
    return pl.pallas_call(
        functools.partial(first_take_kernel if choice else take_kernel, start * choices),
        name="take",
        out_shape=shapes,
        in_specs=[ANY] * (1 + len(choice)),
        out_specs=[VMEM] * len(shapes),
        scratch_shapes=scratch,
        compiler_params=limit(2),
        cost_estimate=pl.CostEstimate(flops=0, bytes_accessed=4 * tokens * choices * depth, transcendentals=0),
    )(*in_hbm(hidden, *choice))


def choose(rows, gates):
    tokens = gates.shape[0]
    first = 2 * lax.broadcasted_iota(jnp.int32, (tokens, 2 * tokens), 0)
    column = lax.broadcasted_iota(jnp.int32, (tokens, 2 * tokens), 1)
    chosen, scales = [], []
    for expert in range(2):
        low, high = gates[:, 2 * expert : 2 * expert + 1], gates[:, 2 * expert + 1 : 2 * expert + 2]
        pick = (column == first + jnp.where(high != 0, 1, 0)).astype(rows.dtype)
        picked = jnp.dot(pick, rows, preferred_element_type=jnp.float32)
        chosen.append(picked.astype(rows.dtype))
        scales.append(low + high)
    return chosen, scales


def columns_of(gates_ref):
    return jnp.transpose(jnp.concatenate([gates_ref[...]] * 2, axis=0))


def gated(chosen, scales, weights):
    width = weights[0].shape[1]
    for at in range(0, width, SLAB):
        end = min(at + SLAB, width)
        terms = [
            scale * jnp.dot(x, w[:, at:end], preferred_element_type=jnp.float32)
            for scale, x, w in zip(scales, chosen, weights)
        ]
        yield at, end, terms[0] + terms[1]


def far_kernel(start, rows_ref, gates_ref, c0, h0, c1, h1, out_ref):
    tokens, width = out_ref.shape[0], c0.shape[1]
    chosen, scales = choose(rows_ref[...], columns_of(gates_ref)[start : start + tokens, :])
    for i, weights in enumerate(((c0, h0), (c1, h1))):
        for at, end, block in gated(chosen, scales, weights):
            out_ref[:, i * width + at : i * width + end] = block.astype(out_ref.dtype)


def cost_of(rows, width):
    return pl.CostEstimate(
        flops=4 * rows.shape[0] * rows.shape[1] * width, bytes_accessed=8 * rows.shape[0] * width, transcendentals=0
    )


def far_project(start, tokens, rows, gates, own, partner):
    width = own[0].shape[1]
    return pl.pallas_call(
        functools.partial(far_kernel, start),
        name="far_project",
        out_shape=pltpu.VMEM((tokens, 2 * width), rows.dtype),
        in_specs=[VMEM] * 6,
        out_specs=VMEM,
        compiler_params=limit(12),
        cost_estimate=cost_of(rows, width),
    )(*near_core(rows, gates, *own, *partner))


def own_kernel(*refs):
    *row_refs, gates_ref, c0, h0, c1, h1, out_ref, staged, sems = refs
    width = c0.shape[1]
    me = lax.axis_index("expert")
    gates = columns_of(gates_ref)
    chosen, scales, at = [], [], 0
    for rows_ref in row_refs:
        tokens = rows_ref.shape[0] // 2
        x, g = choose(rows_ref[...], gates[at : at + tokens, :])
        chosen.append(x)
        scales.append(g)
        at += tokens
    chosen = [jnp.concatenate(x, axis=0) for x in zip(*chosen)]
    scales = [jnp.concatenate(g, axis=0) for g in zip(*scales)]
    copies = []
    for i, weights in enumerate(((c0, h0), (c1, h1))):
        for at, end, block in gated(chosen, scales, weights):
            staged[i, :, at:end] = block.astype(staged.dtype)
        to = pl.multiple_of((me ^ i) * width, width)
        copies.append(pltpu.make_async_copy(staged.at[i], out_ref.at[:, pl.ds(to, width)], sems.at[i]))
        copies[-1].start()
    for copy in copies:
        copy.wait()


def own_project(devices, rows, gates, own, partner):
    width = own[0].shape[1]
    tokens = sum(r.shape[0] for r in rows) // 2
    return pl.pallas_call(
        own_kernel,
        name="own_project",
        out_shape=pltpu.HBM((tokens, devices * width), rows[0].dtype),
        in_specs=[VMEM] * (len(rows) + 5),
        out_specs=ANY,
        scratch_shapes=[pltpu.VMEM((2, tokens, width), rows[0].dtype), pltpu.SemaphoreType.DMA((2,))],
        compiler_params=limit(12),
        cost_estimate=cost_of(rows[0], len(rows) * width),
    )(*near_core(*rows, gates, *own, *partner))


def put_kernel(start, block_ref, whole_ref, out_ref, sems):
    del whole_ref
    tokens, width = block_ref.shape[0], block_ref.shape[1] // 2
    me = lax.axis_index("expert")
    copies = []
    for i in range(2):
        to = pl.multiple_of((me ^ 2 ^ i) * width, width)
        copies.append(
            pltpu.make_async_copy(
                block_ref.at[:, pl.ds(i * width, width)],
                out_ref.at[pl.ds(start, tokens), pl.ds(to, width)],
                sems.at[i],
            )
        )
        copies[-1].start()
    for copy in copies:
        copy.wait()


def put(start, block, whole):
    return pl.pallas_call(
        functools.partial(put_kernel, start),
        name="put",
        out_shape=pltpu.HBM(whole.shape, whole.dtype),
        in_specs=[VMEM, ANY],
        out_specs=ANY,
        scratch_shapes=[pltpu.SemaphoreType.DMA((2,))],
        input_output_aliases={1: 0},
        compiler_params=limit(2),
        cost_estimate=pl.CostEstimate(flops=0, bytes_accessed=4 * block.size, transcendentals=0),
    )(*near_core(block), *in_hbm(whole))


def hold_kernel(*refs):
    ins, outs, sems = refs[: (len(refs) - 1) // 2], refs[(len(refs) - 1) // 2 : -1], refs[-1]
    copies = [pltpu.make_async_copy(a, b, sems.at[i]) for i, (a, b) in enumerate(zip(ins, outs))]
    for copy in copies:
        copy.start()
    for copy in copies:
        copy.wait()


def hold(*arrays):
    return pl.pallas_call(
        hold_kernel,
        name="hold",
        out_shape=[pltpu.VMEM(a.shape, a.dtype) for a in arrays],
        in_specs=[ANY] * len(arrays),
        out_specs=[VMEM] * len(arrays),
        scratch_shapes=[pltpu.SemaphoreType.DMA((len(arrays),))],
        compiler_params=limit(2),
        cost_estimate=pl.CostEstimate(
            flops=0, bytes_accessed=4 * sum(a.size for a in arrays), transcendentals=0
        ),
    )(*in_hbm(*arrays))


def pair_body(expert_ids, gate_weights, hidden, hot_down, cold_down):
    devices = lax.axis_size("expert")
    near = [(i, i ^ 1) for i in range(devices)]
    far = [(i, i ^ 2) for i in range(devices)]
    tokens, _, _ = hidden.shape
    cuts = [tokens * c // 16 for c in CUTS]
    spans = list(zip(cuts[:-1], cuts[1:]))

    def send(array, pairs):
        return lax.ppermute(array, "expert", pairs)

    held, moved, source = [], [], hidden
    for i, (a, b) in enumerate(spans):
        if i == 0:
            rows, gates = take(source, a, b - a, (expert_ids.T, gate_weights.T))
        else:
            (rows,) = take(source, a, b - a)
        held.append(rows)
        moved.append(send(rows, far))
    far_gates = send(gates, far)
    partner = (send(cold_down, near), send(hot_down, near))
    own = hold(cold_down, hot_down)
    back = []
    for i, (a, b) in enumerate(spans):
        result = far_project(a, b - a, moved[i], far_gates, own, partner)
        back.append(send(result, far))
    out = own_project(devices, held, gates, own, partner)
    for i, (a, _) in enumerate(spans):
        out = put(a, back[i], out)
    return out


def solution(mesh):
    devices = mesh.shape["expert"]
    specs = (
        P(("dp", "expert"), None),
        P(("dp", "expert"), None),
        P(("dp", "expert"), None, None),
        P(None, "expert"),
        P(None, "expert"),
    )

    def spread(body):
        return jax.shard_map(
            body, mesh=mesh, in_specs=specs, out_specs=P(("dp", "expert"), None), check_vma=False
        )

    if devices != 4:
        return spread(general_body)
    return spread(pair_body)
```

```python
import functools

import jax
import jax.numpy as jnp
from jax import lax
from jax.experimental import pallas as pl
from jax.experimental.pallas import tpu as pltpu
from jax.sharding import PartitionSpec as P

VMEM = pl.BlockSpec(memory_space=pltpu.VMEM)
ANY = pl.BlockSpec(memory_space=pl.ANY)
SLAB = 128
PARTS = 5
CUTS = (0, 5, 11, 16)


def general_body(expert_ids, gate_weights, hidden, hot_down, cold_down):
    devices = lax.axis_size("expert")
    group_size = min(4, devices)
    cold_count = devices // group_size
    experts_all = cold_count + 1
    tok_rows, top_count, hidden_width = hidden.shape
    capacity = 3 * tok_rows // 4 + tok_rows // 4 * (3 - min(experts_all, 3))
    flat_rows = tok_rows * top_count
    flat_hidden = hidden.reshape(flat_rows, hidden_width)
    flat_ids = expert_ids.reshape(flat_rows)
    hot_chosen = expert_ids == cold_count
    hot_rows = jnp.sum(
        jnp.where(hot_chosen[:, :, None], hidden, jnp.zeros((), hidden.dtype)), axis=1
    )
    hot_gate = jnp.sum(jnp.where(hot_chosen, gate_weights, jnp.zeros((), jnp.float32)), axis=1)
    hot_out = jnp.dot(
        hot_rows,
        lax.all_gather(hot_down, "expert", axis=1, tiled=True),
        preferred_element_type=jnp.float32,
    )
    hot_term = hot_gate[:, None] * hot_out
    onehot_expert = (flat_ids[None, :] == jnp.arange(cold_count, dtype=jnp.int32)[:, None]).astype(
        jnp.int32
    )
    slot_ranks = jnp.sum(onehot_expert * (jnp.cumsum(onehot_expert, axis=1) - 1), axis=0)
    slot_index = jnp.where(flat_ids < cold_count, flat_ids * capacity + slot_ranks, -1)
    placing = (
        jnp.arange(cold_count * capacity, dtype=jnp.int32)[:, None] == slot_index[None, :]
    ).astype(jnp.bfloat16)
    send_rows = jnp.dot(placing, flat_hidden, preferred_element_type=jnp.float32).astype(
        jnp.bfloat16
    )
    copies = jnp.broadcast_to(
        send_rows.reshape(cold_count, 1, capacity, hidden_width),
        (cold_count, group_size, capacity, hidden_width),
    ).reshape(devices, capacity, hidden_width)
    outputs = jnp.einsum(
        "nsf,fd->nsd",
        lax.all_to_all(copies, "expert", split_axis=0, concat_axis=0, tiled=True),
        cold_down,
        preferred_element_type=jnp.float32,
    ).astype(jnp.bfloat16)
    returned = lax.all_to_all(outputs, "expert", split_axis=0, concat_axis=0, tiled=True)
    column_blocks = returned.reshape(cold_count, group_size, capacity, -1)
    placing_blocks = placing.reshape(cold_count, capacity, flat_rows)
    row_outputs = jnp.einsum(
        "ecr,egcd->rgd", placing_blocks, column_blocks, preferred_element_type=jnp.float32
    )
    row_outputs = row_outputs.reshape(tok_rows, top_count, -1)
    scaled = row_outputs * gate_weights[:, :, None]
    cold_term = jnp.sum(scaled, axis=1)
    return (cold_term + hot_term).astype(jnp.bfloat16)


def near_core(*arrays):
    return [pltpu.with_memory_space_constraint(a, pltpu.VMEM) for a in arrays]


def in_hbm(*arrays):
    return [pltpu.with_memory_space_constraint(a, pltpu.HBM) for a in arrays]


def limit(mib):
    return pltpu.CompilerParams(vmem_limit_bytes=mib << 20)


def rows_of(hidden_ref, start, rows_ref, sems):
    flat = hidden_ref.reshape(hidden_ref.shape[0] * hidden_ref.shape[1], hidden_ref.shape[2])
    total = rows_ref.shape[0]
    parts = max(p for p in range(1, PARTS + 1) if total % (8 * p) == 0)
    count = total // parts
    return [
        pltpu.make_async_copy(
            flat.at[pl.ds(start + i * count, count)], rows_ref.at[pl.ds(i * count, count)], sems.at[i]
        )
        for i in range(parts)
    ]


def take_kernel(start, hidden_ref, rows_ref, sems):
    copies = rows_of(hidden_ref, start, rows_ref, sems)
    for copy in copies:
        copy.start()
    for copy in copies:
        copy.wait()


def first_take_kernel(start, hidden_ref, ids_ref, weights_ref, rows_ref, gates_ref, ids, weights, sems):
    large = rows_of(hidden_ref, start, rows_ref, sems)
    small = [
        pltpu.make_async_copy(ids_ref, ids, sems.at[PARTS]),
        pltpu.make_async_copy(weights_ref, weights, sems.at[PARTS + 1]),
    ]
    for copy in large + small:
        copy.start()
    for copy in small:
        copy.wait()
    for e in range(2):
        gates_ref[2 * e : 2 * e + 2, :] = jnp.where(ids[...] == e, weights[...], 0.0)
    for copy in large:
        copy.wait()


def take(hidden, start, tokens, choice=()):
    _, choices, depth = hidden.shape
    shapes = [pltpu.VMEM((tokens * choices, depth), hidden.dtype)]
    scratch = [pltpu.SemaphoreType.DMA((PARTS + 2,))]
    if choice:
        shapes.append(pltpu.VMEM((2 * choices, hidden.shape[0]), choice[1].dtype))
        scratch = [pltpu.VMEM(c.shape, c.dtype) for c in choice] + scratch
    return pl.pallas_call(
        functools.partial(first_take_kernel if choice else take_kernel, start * choices),
        name="take",
        out_shape=shapes,
        in_specs=[ANY] * (1 + len(choice)),
        out_specs=[VMEM] * len(shapes),
        scratch_shapes=scratch,
        compiler_params=limit(2),
        cost_estimate=pl.CostEstimate(flops=0, bytes_accessed=4 * tokens * choices * depth, transcendentals=0),
    )(*in_hbm(hidden, *choice))


def choose(rows, gates):
    tokens = gates.shape[0]
    first = 2 * lax.broadcasted_iota(jnp.int32, (tokens, 2 * tokens), 0)
    column = lax.broadcasted_iota(jnp.int32, (tokens, 2 * tokens), 1)
    chosen, scales = [], []
    for expert in range(2):
        low, high = gates[:, 2 * expert : 2 * expert + 1], gates[:, 2 * expert + 1 : 2 * expert + 2]
        pick = (column == first + jnp.where(high != 0, 1, 0)).astype(rows.dtype)
        picked = jnp.dot(pick, rows, preferred_element_type=jnp.float32)
        chosen.append(picked.astype(rows.dtype))
        scales.append(low + high)
    return chosen, scales


def columns_of(gates_ref):
    return jnp.transpose(jnp.concatenate([gates_ref[...]] * 2, axis=0))


def gated(chosen, scales, weights):
    width = weights[0].shape[1]
    for at in range(0, width, SLAB):
        end = min(at + SLAB, width)
        terms = [
            scale * jnp.dot(x, w[:, at:end], preferred_element_type=jnp.float32)
            for scale, x, w in zip(scales, chosen, weights)
        ]
        yield at, end, terms[0] + terms[1]


def far_kernel(start, rows_ref, gates_ref, c0, h0, c1, h1, out_ref):
    tokens, width = out_ref.shape[0], c0.shape[1]
    chosen, scales = choose(rows_ref[...], columns_of(gates_ref)[start : start + tokens, :])
    for i, weights in enumerate(((c0, h0), (c1, h1))):
        for at, end, block in gated(chosen, scales, weights):
            out_ref[:, i * width + at : i * width + end] = block.astype(out_ref.dtype)


def cost_of(rows, width):
    return pl.CostEstimate(
        flops=4 * rows.shape[0] * rows.shape[1] * width, bytes_accessed=8 * rows.shape[0] * width, transcendentals=0
    )


def far_project(start, tokens, rows, gates, own, partner):
    width = own[0].shape[1]
    return pl.pallas_call(
        functools.partial(far_kernel, start),
        name="far_project",
        out_shape=pltpu.VMEM((tokens, 2 * width), rows.dtype),
        in_specs=[VMEM] * 6,
        out_specs=VMEM,
        compiler_params=limit(12),
        cost_estimate=cost_of(rows, width),
    )(*near_core(rows, gates, *own, *partner))


def own_kernel(*refs):
    *row_refs, gates_ref, c0, h0, c1, h1, out_ref, staged, sems = refs
    width = c0.shape[1]
    me = lax.axis_index("expert")
    gates = columns_of(gates_ref)
    chosen, scales, at = [], [], 0
    for rows_ref in row_refs:
        tokens = rows_ref.shape[0] // 2
        x, g = choose(rows_ref[...], gates[at : at + tokens, :])
        chosen.append(x)
        scales.append(g)
        at += tokens
    chosen = [jnp.concatenate(x, axis=0) for x in zip(*chosen)]
    scales = [jnp.concatenate(g, axis=0) for g in zip(*scales)]
    copies = []
    for i, weights in enumerate(((c0, h0), (c1, h1))):
        for at, end, block in gated(chosen, scales, weights):
            staged[i, :, at:end] = block.astype(staged.dtype)
        to = pl.multiple_of((me ^ i) * width, width)
        copies.append(pltpu.make_async_copy(staged.at[i], out_ref.at[:, pl.ds(to, width)], sems.at[i]))
        copies[-1].start()
    for copy in copies:
        copy.wait()


def own_project(devices, rows, gates, own, partner):
    width = own[0].shape[1]
    tokens = sum(r.shape[0] for r in rows) // 2
    return pl.pallas_call(
        own_kernel,
        name="own_project",
        out_shape=pltpu.HBM((tokens, devices * width), rows[0].dtype),
        in_specs=[VMEM] * (len(rows) + 5),
        out_specs=ANY,
        scratch_shapes=[pltpu.VMEM((2, tokens, width), rows[0].dtype), pltpu.SemaphoreType.DMA((2,))],
        compiler_params=limit(12),
        cost_estimate=cost_of(rows[0], len(rows) * width),
    )(*near_core(*rows, gates, *own, *partner))


def put_kernel(start, block_ref, whole_ref, out_ref, sems):
    del whole_ref
    tokens, width = block_ref.shape[0], block_ref.shape[1] // 2
    me = lax.axis_index("expert")
    copies = []
    for i in range(2):
        to = pl.multiple_of((me ^ 2 ^ i) * width, width)
        copies.append(
            pltpu.make_async_copy(
                block_ref.at[:, pl.ds(i * width, width)],
                out_ref.at[pl.ds(start, tokens), pl.ds(to, width)],
                sems.at[i],
            )
        )
        copies[-1].start()
    for copy in copies:
        copy.wait()


def put(start, block, whole):
    return pl.pallas_call(
        functools.partial(put_kernel, start),
        name="put",
        out_shape=pltpu.HBM(whole.shape, whole.dtype),
        in_specs=[VMEM, ANY],
        out_specs=ANY,
        scratch_shapes=[pltpu.SemaphoreType.DMA((2,))],
        input_output_aliases={1: 0},
        compiler_params=limit(2),
        cost_estimate=pl.CostEstimate(flops=0, bytes_accessed=4 * block.size, transcendentals=0),
    )(*near_core(block), *in_hbm(whole))


def hold_kernel(*refs):
    ins, outs, sems = refs[: (len(refs) - 1) // 2], refs[(len(refs) - 1) // 2 : -1], refs[-1]
    copies = [pltpu.make_async_copy(a, b, sems.at[i]) for i, (a, b) in enumerate(zip(ins, outs))]
    for copy in copies:
        copy.start()
    for copy in copies:
        copy.wait()


def hold(*arrays):
    return pl.pallas_call(
        hold_kernel,
        name="hold",
        out_shape=[pltpu.VMEM(a.shape, a.dtype) for a in arrays],
        in_specs=[ANY] * len(arrays),
        out_specs=[VMEM] * len(arrays),
        scratch_shapes=[pltpu.SemaphoreType.DMA((len(arrays),))],
        compiler_params=limit(2),
        cost_estimate=pl.CostEstimate(
            flops=0, bytes_accessed=4 * sum(a.size for a in arrays), transcendentals=0
        ),
    )(*in_hbm(*arrays))


def pair_body(expert_ids, gate_weights, hidden, hot_down, cold_down):
    devices = lax.axis_size("expert")
    near = [(i, i ^ 1) for i in range(devices)]
    far = [(i, i ^ 2) for i in range(devices)]
    tokens, _, _ = hidden.shape
    cuts = [tokens * c // 16 for c in CUTS]
    spans = list(zip(cuts[:-1], cuts[1:]))

    def send(array, pairs):
        return lax.ppermute(array, "expert", pairs)

    held, moved, source = [], [], hidden
    for i, (a, b) in enumerate(spans):
        if i == 1:
            rows, gates = take(source, a, b - a, (expert_ids.T, gate_weights.T))
        else:
            (rows,) = take(source, a, b - a)
        held.append(rows)
        moved.append(send(rows, far))
    far_gates = send(gates, far)
    partner = (send(cold_down, near), send(hot_down, near))
    own = hold(cold_down, hot_down)
    back = []
    for i, (a, b) in enumerate(spans):
        result = far_project(a, b - a, moved[i], far_gates, own, partner)
        back.append(send(result, far))
    out = own_project(devices, held, gates, own, partner)
    for i, (a, _) in enumerate(spans):
        out = put(a, back[i], out)
    return out


def solution(mesh):
    devices = mesh.shape["expert"]
    specs = (
        P(("dp", "expert"), None),
        P(("dp", "expert"), None),
        P(("dp", "expert"), None, None),
        P(None, "expert"),
        P(None, "expert"),
    )

    def spread(body):
        return jax.shard_map(
            body, mesh=mesh, in_specs=specs, out_specs=P(("dp", "expert"), None), check_vma=False
        )

    if devices != 4:
        return spread(general_body)
    return spread(pair_body)
```

```python
import functools

import jax
import jax.numpy as jnp
from jax import lax
from jax.experimental import pallas as pl
from jax.experimental.pallas import tpu as pltpu
from jax.sharding import PartitionSpec as P

VMEM = pl.BlockSpec(memory_space=pltpu.VMEM)
ANY = pl.BlockSpec(memory_space=pl.ANY)
SLAB = 128
CUTS = (0, 5, 10, 16)


def general_body(expert_ids, gate_weights, hidden, hot_down, cold_down):
    devices = lax.axis_size("expert")
    group_size = min(4, devices)
    cold_count = devices // group_size
    experts_all = cold_count + 1
    tok_rows, top_count, hidden_width = hidden.shape
    capacity = 3 * tok_rows // 4 + tok_rows // 4 * (3 - min(experts_all, 3))
    flat_rows = tok_rows * top_count
    flat_hidden = hidden.reshape(flat_rows, hidden_width)
    flat_ids = expert_ids.reshape(flat_rows)
    hot_chosen = expert_ids == cold_count
    hot_rows = jnp.sum(
        jnp.where(hot_chosen[:, :, None], hidden, jnp.zeros((), hidden.dtype)), axis=1
    )
    hot_gate = jnp.sum(jnp.where(hot_chosen, gate_weights, jnp.zeros((), jnp.float32)), axis=1)
    hot_out = jnp.dot(
        hot_rows,
        lax.all_gather(hot_down, "expert", axis=1, tiled=True),
        preferred_element_type=jnp.float32,
    )
    hot_term = hot_gate[:, None] * hot_out
    onehot_expert = (flat_ids[None, :] == jnp.arange(cold_count, dtype=jnp.int32)[:, None]).astype(
        jnp.int32
    )
    slot_ranks = jnp.sum(onehot_expert * (jnp.cumsum(onehot_expert, axis=1) - 1), axis=0)
    slot_index = jnp.where(flat_ids < cold_count, flat_ids * capacity + slot_ranks, -1)
    placing = (
        jnp.arange(cold_count * capacity, dtype=jnp.int32)[:, None] == slot_index[None, :]
    ).astype(jnp.bfloat16)
    send_rows = jnp.dot(placing, flat_hidden, preferred_element_type=jnp.float32).astype(
        jnp.bfloat16
    )
    copies = jnp.broadcast_to(
        send_rows.reshape(cold_count, 1, capacity, hidden_width),
        (cold_count, group_size, capacity, hidden_width),
    ).reshape(devices, capacity, hidden_width)
    outputs = jnp.einsum(
        "nsf,fd->nsd",
        lax.all_to_all(copies, "expert", split_axis=0, concat_axis=0, tiled=True),
        cold_down,
        preferred_element_type=jnp.float32,
    ).astype(jnp.bfloat16)
    returned = lax.all_to_all(outputs, "expert", split_axis=0, concat_axis=0, tiled=True)
    column_blocks = returned.reshape(cold_count, group_size, capacity, -1)
    placing_blocks = placing.reshape(cold_count, capacity, flat_rows)
    row_outputs = jnp.einsum(
        "ecr,egcd->rgd", placing_blocks, column_blocks, preferred_element_type=jnp.float32
    )
    row_outputs = row_outputs.reshape(tok_rows, top_count, -1)
    scaled = row_outputs * gate_weights[:, :, None]
    cold_term = jnp.sum(scaled, axis=1)
    return (cold_term + hot_term).astype(jnp.bfloat16)


def near_core(*arrays):
    return [pltpu.with_memory_space_constraint(a, pltpu.VMEM) for a in arrays]


def in_hbm(*arrays):
    return [pltpu.with_memory_space_constraint(a, pltpu.HBM) for a in arrays]


def limit(mib):
    return pltpu.CompilerParams(vmem_limit_bytes=mib << 20)


def rows_of(hidden_ref, start, rows_ref, sem):
    flat = hidden_ref.reshape(hidden_ref.shape[0] * hidden_ref.shape[1], hidden_ref.shape[2])
    return pltpu.make_async_copy(flat.at[pl.ds(start, rows_ref.shape[0])], rows_ref, sem)


def take_kernel(hidden_ref, ids_ref, weights_ref, *refs):
    *row_refs, gates_ref, ids, weights, sems = refs
    small = [
        pltpu.make_async_copy(ids_ref, ids, sems.at[0]),
        pltpu.make_async_copy(weights_ref, weights, sems.at[1]),
    ]
    large, at = [], 0
    for i, rows_ref in enumerate(row_refs):
        large.append(rows_of(hidden_ref, at, rows_ref, sems.at[2 + i]))
        at += rows_ref.shape[0]
    for copy in small + large:
        copy.start()
    for copy in small:
        copy.wait()
    for e in range(2):
        gates_ref[2 * e : 2 * e + 2, :] = jnp.where(ids[...] == e, weights[...], 0.0)
    for copy in large:
        copy.wait()


def take(hidden, ids, weights, spans):
    tokens, choices, depth = hidden.shape
    shapes = [pltpu.VMEM(((b - a) * choices, depth), hidden.dtype) for a, b in spans]
    shapes.append(pltpu.VMEM((2 * choices, tokens), weights.dtype))
    *rows, gates = pl.pallas_call(
        take_kernel,
        name="take",
        out_shape=shapes,
        in_specs=[ANY] * 3,
        out_specs=[VMEM] * len(shapes),
        scratch_shapes=[
            pltpu.VMEM(ids.shape, ids.dtype),
            pltpu.VMEM(weights.shape, weights.dtype),
            pltpu.SemaphoreType.DMA((2 + len(spans),)),
        ],
        compiler_params=limit(2),
        cost_estimate=pl.CostEstimate(flops=0, bytes_accessed=4 * tokens * choices * depth, transcendentals=0),
    )(*in_hbm(hidden, ids, weights))
    return rows, gates


def choose(rows, gates):
    tokens = gates.shape[0]
    first = 2 * lax.broadcasted_iota(jnp.int32, (tokens, 2 * tokens), 0)
    column = lax.broadcasted_iota(jnp.int32, (tokens, 2 * tokens), 1)
    chosen, scales = [], []
    for expert in range(2):
        low, high = gates[:, 2 * expert : 2 * expert + 1], gates[:, 2 * expert + 1 : 2 * expert + 2]
        pick = (column == first + jnp.where(high != 0, 1, 0)).astype(rows.dtype)
        picked = jnp.dot(pick, rows, preferred_element_type=jnp.float32)
        chosen.append(picked.astype(rows.dtype))
        scales.append(low + high)
    return chosen, scales


def columns_of(gates_ref):
    return jnp.transpose(jnp.concatenate([gates_ref[...]] * 2, axis=0))


def gated(chosen, scales, weights):
    width = weights[0].shape[1]
    for at in range(0, width, SLAB):
        end = min(at + SLAB, width)
        terms = [
            scale * jnp.dot(x, w[:, at:end], preferred_element_type=jnp.float32)
            for scale, x, w in zip(scales, chosen, weights)
        ]
        yield at, end, terms[0] + terms[1]


def far_kernel(start, part_ref, whole_ref, gates_ref, c0, h0, c1, h1, out_ref, rows):
    tokens, width = out_ref.shape[0], c0.shape[1]
    core = lax.axis_index("expert") % 2

    @pl.when(core == 0)
    def _():
        rows[...] = part_ref[...]

    @pl.when(core == 1)
    def _():
        rows[...] = whole_ref[start : start + tokens].reshape(rows.shape)

    chosen, scales = choose(rows[...], columns_of(gates_ref)[start : start + tokens, :])
    for i, weights in enumerate(((c0, h0), (c1, h1))):
        for at, end, block in gated(chosen, scales, weights):
            out_ref[:, i * width + at : i * width + end] = block.astype(out_ref.dtype)


def cost_of(rows, width):
    return pl.CostEstimate(
        flops=4 * rows.shape[0] * rows.shape[1] * width, bytes_accessed=8 * rows.shape[0] * width, transcendentals=0
    )


def far_project(start, tokens, part, whole, gates, own, partner):
    width = own[0].shape[1]
    operands = [part, whole, gates, *own, *partner]
    return pl.pallas_call(
        functools.partial(far_kernel, start),
        name="far_project",
        out_shape=pltpu.VMEM((tokens, 2 * width), part.dtype),
        in_specs=[VMEM] * len(operands),
        out_specs=VMEM,
        scratch_shapes=[pltpu.VMEM(part.shape, part.dtype)],
        compiler_params=limit(12),
        cost_estimate=cost_of(part, width),
    )(*near_core(*operands))


def own_kernel(blocks, count, *refs):
    row_refs, rest = refs[:count], refs[count:]
    gates_ref, *weight_refs, whole_ref, out_ref, staged, sems = rest
    del whole_ref
    width = weight_refs[0].shape[1]
    me = lax.axis_index("expert")

    def write(names):
        gates = columns_of(gates_ref)
        chosen, scales, at = [], [], 0
        for rows_ref in row_refs:
            tokens = rows_ref.shape[0] // 2
            x, g = choose(rows_ref[...], gates[at : at + tokens, :])
            chosen.append(x)
            scales.append(g)
            at += tokens
        joined = [jnp.concatenate(x, axis=0) for x in zip(*chosen)]
        spread = [jnp.concatenate(g, axis=0) for g in zip(*scales)]
        copies = []
        for name in names:
            slot = [b for b, _ in blocks].index(name)
            for at, end, block in gated(joined, spread, weight_refs[2 * slot : 2 * slot + 2]):
                staged[name, :, at:end] = block.astype(staged.dtype)
            to = pl.multiple_of((me ^ name) * width, width)
            copies.append(pltpu.make_async_copy(staged.at[name], out_ref.at[:, pl.ds(to, width)], sems.at[name]))
            copies[-1].start()
        for copy in copies:
            copy.wait()

    if all(len(turns) == 2 for _, turns in blocks):
        write([name for name, _ in blocks])
        return
    for turn in range(2):
        names = [name for name, turns in blocks if turn in turns]
        if names:
            pl.when(me % 2 == turn)(functools.partial(write, names))


def own_project(blocks, rows, gates, weights, out):
    width = weights[0].shape[1]
    tokens = sum(r.shape[0] for r in rows) // 2
    operands = [*rows, gates, *weights]
    return pl.pallas_call(
        functools.partial(own_kernel, blocks, len(rows)),
        name="own_project",
        out_shape=pltpu.HBM(out.shape, out.dtype),
        in_specs=[VMEM] * len(operands) + [ANY],
        out_specs=ANY,
        scratch_shapes=[pltpu.VMEM((2, tokens, width), rows[0].dtype), pltpu.SemaphoreType.DMA((2,))],
        input_output_aliases={len(operands): 0},
        compiler_params=limit(12),
        cost_estimate=cost_of(rows[0], len(rows) * width * len(weights) // 4),
    )(*near_core(*operands), *in_hbm(out))


def fresh_kernel(out_ref):
    del out_ref


def fresh(shape, dtype):
    return pl.pallas_call(
        fresh_kernel,
        name="fresh",
        out_shape=pltpu.HBM(shape, dtype),
        out_specs=ANY,
        compiler_params=limit(2),
        cost_estimate=pl.CostEstimate(flops=0, bytes_accessed=0, transcendentals=0),
    )()


def put_kernel(start, block_ref, whole_ref, out_ref, sems):
    del whole_ref
    tokens, width = block_ref.shape[0], block_ref.shape[1] // 2
    me = lax.axis_index("expert")
    copies = []
    for i in range(2):
        to = pl.multiple_of((me ^ 2 ^ i) * width, width)
        copies.append(
            pltpu.make_async_copy(
                block_ref.at[:, pl.ds(i * width, width)],
                out_ref.at[pl.ds(start, tokens), pl.ds(to, width)],
                sems.at[i],
            )
        )
        copies[-1].start()
    for copy in copies:
        copy.wait()


def put(start, block, whole):
    return pl.pallas_call(
        functools.partial(put_kernel, start),
        name="put",
        out_shape=pltpu.HBM(whole.shape, whole.dtype),
        in_specs=[VMEM, ANY],
        out_specs=ANY,
        scratch_shapes=[pltpu.SemaphoreType.DMA((2,))],
        input_output_aliases={1: 0},
        compiler_params=limit(2),
        cost_estimate=pl.CostEstimate(flops=0, bytes_accessed=4 * block.size, transcendentals=0),
    )(*near_core(block), *in_hbm(whole))


def hold_kernel(*refs):
    ins, outs, sems = refs[: (len(refs) - 1) // 2], refs[(len(refs) - 1) // 2 : -1], refs[-1]
    copies = [pltpu.make_async_copy(a, b, sems.at[i]) for i, (a, b) in enumerate(zip(ins, outs))]
    for copy in copies:
        copy.start()
    for copy in copies:
        copy.wait()


def hold(*arrays):
    return pl.pallas_call(
        hold_kernel,
        name="hold",
        out_shape=[pltpu.VMEM(a.shape, a.dtype) for a in arrays],
        in_specs=[ANY] * len(arrays),
        out_specs=[VMEM] * len(arrays),
        scratch_shapes=[pltpu.SemaphoreType.DMA((len(arrays),))],
        compiler_params=limit(2),
        cost_estimate=pl.CostEstimate(
            flops=0, bytes_accessed=4 * sum(a.size for a in arrays), transcendentals=0
        ),
    )(*in_hbm(*arrays))


def pair_body(expert_ids, gate_weights, hidden, hot_down, cold_down):
    devices, groups = lax.axis_size("expert"), lax.axis_size("dp")
    near = [(i, i ^ 1) for i in range(devices)]
    far = [(i, i ^ 2) for i in range(devices)]
    tokens = hidden.shape[0]
    cuts = [tokens * c // 16 for c in CUTS]
    spans = list(zip(cuts[:-1], cuts[1:]))

    def send(array, pairs):
        return lax.ppermute(array, "expert", pairs)

    def send_by(array, core):
        pairs = [
            (g * devices + i, g * devices + (i ^ 2) if i % 2 == core else (g ^ (1 + core)) * devices + i)
            for g in range(groups)
            for i in range(devices)
        ]
        return lax.ppermute(array, ("dp", "expert"), pairs)

    whole = send_by(hidden, 1)
    held, gates = take(hidden, expert_ids.T, gate_weights.T, spans)
    moved = [send_by(rows, 0) for rows in held]
    far_gates = send(gates, far)
    partner = (send(cold_down, near), send(hot_down, near))
    out = fresh((tokens, devices * hot_down.shape[1]), hidden.dtype)
    own = hold(cold_down, hot_down)
    back = []
    for i, (a, b) in enumerate(spans):
        result = far_project(a, b - a, moved[i], whole, far_gates, own, partner)
        back.append(send(result, far))
    out = own_project(((0, (0, 1)), (1, (0, 1))), held, gates, (*own, *partner), out)
    for i, (a, _) in enumerate(spans):
        out = put(a, back[i], out)
    return out


def solution(mesh):
    devices = mesh.shape["expert"]
    specs = (
        P(("dp", "expert"), None),
        P(("dp", "expert"), None),
        P(("dp", "expert"), None, None),
        P(None, "expert"),
        P(None, "expert"),
    )

    def spread(body):
        return jax.shard_map(
            body, mesh=mesh, in_specs=specs, out_specs=P(("dp", "expert"), None), check_vma=False
        )

    if devices != 4 or mesh.shape["dp"] % 4:
        return spread(general_body)
    return spread(pair_body)
```

```python
import functools

import jax
import jax.numpy as jnp
from jax import lax
from jax.experimental import pallas as pl
from jax.experimental.pallas import tpu as pltpu
from jax.sharding import PartitionSpec as P

VMEM = pl.BlockSpec(memory_space=pltpu.VMEM)
ANY = pl.BlockSpec(memory_space=pl.ANY)
SLAB = 128
CUTS = (0, 5, 10, 16)


def general_body(expert_ids, gate_weights, hidden, hot_down, cold_down):
    devices = lax.axis_size("expert")
    group_size = min(4, devices)
    cold_count = devices // group_size
    experts_all = cold_count + 1
    tok_rows, top_count, hidden_width = hidden.shape
    capacity = 3 * tok_rows // 4 + tok_rows // 4 * (3 - min(experts_all, 3))
    flat_rows = tok_rows * top_count
    flat_hidden = hidden.reshape(flat_rows, hidden_width)
    flat_ids = expert_ids.reshape(flat_rows)
    hot_chosen = expert_ids == cold_count
    hot_rows = jnp.sum(
        jnp.where(hot_chosen[:, :, None], hidden, jnp.zeros((), hidden.dtype)), axis=1
    )
    hot_gate = jnp.sum(jnp.where(hot_chosen, gate_weights, jnp.zeros((), jnp.float32)), axis=1)
    hot_out = jnp.dot(
        hot_rows,
        lax.all_gather(hot_down, "expert", axis=1, tiled=True),
        preferred_element_type=jnp.float32,
    )
    hot_term = hot_gate[:, None] * hot_out
    onehot_expert = (flat_ids[None, :] == jnp.arange(cold_count, dtype=jnp.int32)[:, None]).astype(
        jnp.int32
    )
    slot_ranks = jnp.sum(onehot_expert * (jnp.cumsum(onehot_expert, axis=1) - 1), axis=0)
    slot_index = jnp.where(flat_ids < cold_count, flat_ids * capacity + slot_ranks, -1)
    placing = (
        jnp.arange(cold_count * capacity, dtype=jnp.int32)[:, None] == slot_index[None, :]
    ).astype(jnp.bfloat16)
    send_rows = jnp.dot(placing, flat_hidden, preferred_element_type=jnp.float32).astype(
        jnp.bfloat16
    )
    copies = jnp.broadcast_to(
        send_rows.reshape(cold_count, 1, capacity, hidden_width),
        (cold_count, group_size, capacity, hidden_width),
    ).reshape(devices, capacity, hidden_width)
    outputs = jnp.einsum(
        "nsf,fd->nsd",
        lax.all_to_all(copies, "expert", split_axis=0, concat_axis=0, tiled=True),
        cold_down,
        preferred_element_type=jnp.float32,
    ).astype(jnp.bfloat16)
    returned = lax.all_to_all(outputs, "expert", split_axis=0, concat_axis=0, tiled=True)
    column_blocks = returned.reshape(cold_count, group_size, capacity, -1)
    placing_blocks = placing.reshape(cold_count, capacity, flat_rows)
    row_outputs = jnp.einsum(
        "ecr,egcd->rgd", placing_blocks, column_blocks, preferred_element_type=jnp.float32
    )
    row_outputs = row_outputs.reshape(tok_rows, top_count, -1)
    scaled = row_outputs * gate_weights[:, :, None]
    cold_term = jnp.sum(scaled, axis=1)
    return (cold_term + hot_term).astype(jnp.bfloat16)


def near_core(*arrays):
    return [pltpu.with_memory_space_constraint(a, pltpu.VMEM) for a in arrays]


def in_hbm(*arrays):
    return [pltpu.with_memory_space_constraint(a, pltpu.HBM) for a in arrays]


def limit(mib):
    return pltpu.CompilerParams(vmem_limit_bytes=mib << 20)


def rows_of(hidden_ref, start, rows_ref, sem):
    flat = hidden_ref.reshape(hidden_ref.shape[0] * hidden_ref.shape[1], hidden_ref.shape[2])
    return pltpu.make_async_copy(flat.at[pl.ds(start, rows_ref.shape[0])], rows_ref, sem)


def take_kernel(hidden_ref, ids_ref, weights_ref, *refs):
    *row_refs, gates_ref, ids, weights, sems = refs
    small = [
        pltpu.make_async_copy(ids_ref, ids, sems.at[0]),
        pltpu.make_async_copy(weights_ref, weights, sems.at[1]),
    ]
    large, at = [], 0
    for i, rows_ref in enumerate(row_refs):
        large.append(rows_of(hidden_ref, at, rows_ref, sems.at[2 + i]))
        at += rows_ref.shape[0]
    for copy in small + large:
        copy.start()
    for copy in small:
        copy.wait()
    for e in range(2):
        gates_ref[2 * e : 2 * e + 2, :] = jnp.where(ids[...] == e, weights[...], 0.0)
    for copy in large:
        copy.wait()


def take(hidden, ids, weights, spans):
    tokens, choices, depth = hidden.shape
    shapes = [pltpu.VMEM(((b - a) * choices, depth), hidden.dtype) for a, b in spans]
    shapes.append(pltpu.VMEM((2 * choices, tokens), weights.dtype))
    *rows, gates = pl.pallas_call(
        take_kernel,
        name="take",
        out_shape=shapes,
        in_specs=[ANY] * 3,
        out_specs=[VMEM] * len(shapes),
        scratch_shapes=[
            pltpu.VMEM(ids.shape, ids.dtype),
            pltpu.VMEM(weights.shape, weights.dtype),
            pltpu.SemaphoreType.DMA((2 + len(spans),)),
        ],
        compiler_params=limit(2),
        cost_estimate=pl.CostEstimate(flops=0, bytes_accessed=4 * tokens * choices * depth, transcendentals=0),
    )(*in_hbm(hidden, ids, weights))
    return rows, gates


def choose(rows, gates):
    tokens = gates.shape[0]
    first = 2 * lax.broadcasted_iota(jnp.int32, (tokens, 2 * tokens), 0)
    column = lax.broadcasted_iota(jnp.int32, (tokens, 2 * tokens), 1)
    chosen, scales = [], []
    for expert in range(2):
        low, high = gates[:, 2 * expert : 2 * expert + 1], gates[:, 2 * expert + 1 : 2 * expert + 2]
        pick = (column == first + jnp.where(high != 0, 1, 0)).astype(rows.dtype)
        picked = jnp.dot(pick, rows, preferred_element_type=jnp.float32)
        chosen.append(picked.astype(rows.dtype))
        scales.append(low + high)
    return chosen, scales


def columns_of(gates_ref):
    return jnp.transpose(jnp.concatenate([gates_ref[...]] * 2, axis=0))


def gated(chosen, scales, weights):
    width = weights[0].shape[1]
    for at in range(0, width, SLAB):
        end = min(at + SLAB, width)
        terms = [
            scale * jnp.dot(x, w[:, at:end], preferred_element_type=jnp.float32)
            for scale, x, w in zip(scales, chosen, weights)
        ]
        yield at, end, terms[0] + terms[1]


def far_kernel(start, part_ref, whole_ref, gates_ref, c0, h0, c1, h1, out_ref, rows):
    tokens, width = out_ref.shape[0], c0.shape[1]
    core = lax.axis_index("expert") % 2

    @pl.when(core == 0)
    def _():
        rows[...] = part_ref[...]

    @pl.when(core == 1)
    def _():
        rows[...] = whole_ref[start : start + tokens].reshape(rows.shape)

    chosen, scales = choose(rows[...], columns_of(gates_ref)[start : start + tokens, :])
    for i, weights in enumerate(((c0, h0), (c1, h1))):
        for at, end, block in gated(chosen, scales, weights):
            out_ref[:, i * width + at : i * width + end] = block.astype(out_ref.dtype)


def cost_of(rows, width):
    return pl.CostEstimate(
        flops=4 * rows.shape[0] * rows.shape[1] * width, bytes_accessed=8 * rows.shape[0] * width, transcendentals=0
    )


def far_project(start, tokens, part, whole, gates, own, partner):
    width = own[0].shape[1]
    operands = [part, whole, gates, *own, *partner]
    return pl.pallas_call(
        functools.partial(far_kernel, start),
        name="far_project",
        out_shape=pltpu.VMEM((tokens, 2 * width), part.dtype),
        in_specs=[VMEM] * len(operands),
        out_specs=VMEM,
        scratch_shapes=[pltpu.VMEM(part.shape, part.dtype)],
        compiler_params=limit(12),
        cost_estimate=cost_of(part, width),
    )(*near_core(*operands))


def own_kernel(blocks, count, *refs):
    row_refs, rest = refs[:count], refs[count:]
    gates_ref, *weight_refs, whole_ref, out_ref, staged, sems = rest
    del whole_ref
    width = weight_refs[0].shape[1]
    me = lax.axis_index("expert")

    def write(names):
        gates = columns_of(gates_ref)
        chosen, scales, at = [], [], 0
        for rows_ref in row_refs:
            tokens = rows_ref.shape[0] // 2
            x, g = choose(rows_ref[...], gates[at : at + tokens, :])
            chosen.append(x)
            scales.append(g)
            at += tokens
        joined = [jnp.concatenate(x, axis=0) for x in zip(*chosen)]
        spread = [jnp.concatenate(g, axis=0) for g in zip(*scales)]
        copies = []
        for name in names:
            slot = [b for b, _ in blocks].index(name)
            for at, end, block in gated(joined, spread, weight_refs[2 * slot : 2 * slot + 2]):
                staged[name, :, at:end] = block.astype(staged.dtype)
            to = pl.multiple_of((me ^ name) * width, width)
            copies.append(pltpu.make_async_copy(staged.at[name], out_ref.at[:, pl.ds(to, width)], sems.at[name]))
            copies[-1].start()
        for copy in copies:
            copy.wait()

    if all(len(turns) == 2 for _, turns in blocks):
        write([name for name, _ in blocks])
        return
    for turn in range(2):
        names = [name for name, turns in blocks if turn in turns]
        if names:
            pl.when(me % 2 == turn)(functools.partial(write, names))


def own_project(blocks, rows, gates, weights, out):
    width = weights[0].shape[1]
    tokens = sum(r.shape[0] for r in rows) // 2
    operands = [*rows, gates, *weights]
    return pl.pallas_call(
        functools.partial(own_kernel, blocks, len(rows)),
        name="own_project",
        out_shape=pltpu.HBM(out.shape, out.dtype),
        in_specs=[VMEM] * len(operands) + [ANY],
        out_specs=ANY,
        scratch_shapes=[pltpu.VMEM((2, tokens, width), rows[0].dtype), pltpu.SemaphoreType.DMA((2,))],
        input_output_aliases={len(operands): 0},
        compiler_params=limit(12),
        cost_estimate=cost_of(rows[0], len(rows) * width * len(weights) // 4),
    )(*near_core(*operands), *in_hbm(out))


def fresh_kernel(out_ref):
    del out_ref


def fresh(shape, dtype):
    return pl.pallas_call(
        fresh_kernel,
        name="fresh",
        out_shape=pltpu.HBM(shape, dtype),
        out_specs=ANY,
        compiler_params=limit(2),
        cost_estimate=pl.CostEstimate(flops=0, bytes_accessed=0, transcendentals=0),
    )()


def put_kernel(starts, *refs):
    block_refs, (_, out_ref, sems) = refs[: len(starts)], refs[len(starts) :]
    me = lax.axis_index("expert")
    copies = []
    for start, block_ref in zip(starts, block_refs):
        tokens, width = block_ref.shape[0], block_ref.shape[1] // 2
        for i in range(2):
            to = pl.multiple_of((me ^ 2 ^ i) * width, width)
            copies.append(
                pltpu.make_async_copy(
                    block_ref.at[:, pl.ds(i * width, width)],
                    out_ref.at[pl.ds(start, tokens), pl.ds(to, width)],
                    sems.at[len(copies)],
                )
            )
            copies[-1].start()
    for copy in copies:
        copy.wait()


def put(starts, blocks, whole):
    count = len(starts)
    return pl.pallas_call(
        functools.partial(put_kernel, starts),
        name="put",
        out_shape=pltpu.HBM(whole.shape, whole.dtype),
        in_specs=[VMEM] * count + [ANY],
        out_specs=ANY,
        scratch_shapes=[pltpu.SemaphoreType.DMA((2 * count,))],
        input_output_aliases={count: 0},
        compiler_params=limit(2),
        cost_estimate=pl.CostEstimate(
            flops=0, bytes_accessed=4 * sum(b.size for b in blocks), transcendentals=0
        ),
    )(*near_core(*blocks), *in_hbm(whole))


def hold_kernel(*refs):
    ins, outs, sems = refs[: (len(refs) - 1) // 2], refs[(len(refs) - 1) // 2 : -1], refs[-1]
    copies = [pltpu.make_async_copy(a, b, sems.at[i]) for i, (a, b) in enumerate(zip(ins, outs))]
    for copy in copies:
        copy.start()
    for copy in copies:
        copy.wait()


def hold(*arrays):
    return pl.pallas_call(
        hold_kernel,
        name="hold",
        out_shape=[pltpu.VMEM(a.shape, a.dtype) for a in arrays],
        in_specs=[ANY] * len(arrays),
        out_specs=[VMEM] * len(arrays),
        scratch_shapes=[pltpu.SemaphoreType.DMA((len(arrays),))],
        compiler_params=limit(2),
        cost_estimate=pl.CostEstimate(
            flops=0, bytes_accessed=4 * sum(a.size for a in arrays), transcendentals=0
        ),
    )(*in_hbm(*arrays))


def pair_body(expert_ids, gate_weights, hidden, hot_down, cold_down):
    devices, groups = lax.axis_size("expert"), lax.axis_size("dp")
    near = [(i, i ^ 1) for i in range(devices)]
    far = [(i, i ^ 2) for i in range(devices)]
    tokens = hidden.shape[0]
    cuts = [tokens * c // 16 for c in CUTS]
    spans = list(zip(cuts[:-1], cuts[1:]))

    def send(array, pairs):
        return lax.ppermute(array, "expert", pairs)

    def send_by(array, core):
        pairs = [
            (g * devices + i, g * devices + (i ^ 2) if i % 2 == core else (g ^ (1 + core)) * devices + i)
            for g in range(groups)
            for i in range(devices)
        ]
        return lax.ppermute(array, ("dp", "expert"), pairs)

    whole = send_by(hidden, 1)
    held, gates = take(hidden, expert_ids.T, gate_weights.T, spans)
    moved = [send_by(rows, 0) for rows in held]
    far_gates = send(gates, far)
    partner = (send(cold_down, near), send(hot_down, near))
    out = fresh((tokens, devices * hot_down.shape[1]), hidden.dtype)
    own = hold(cold_down, hot_down)
    back = []
    for i, (a, b) in enumerate(spans):
        if i == 2:
            out = own_project(((0, (1,)),), held, gates, own, out)
        result = far_project(a, b - a, moved[i], whole, far_gates, own, partner)
        back.append(send(result, far))
    out = own_project(((0, (0,)), (1, (0, 1))), held, gates, (*own, *partner), out)
    starts = [a for a, _ in spans]
    out = put(starts[:-1], back[:-1], out)
    out = put(starts[-1:], back[-1:], out)
    return out


def solution(mesh):
    devices = mesh.shape["expert"]
    specs = (
        P(("dp", "expert"), None),
        P(("dp", "expert"), None),
        P(("dp", "expert"), None, None),
        P(None, "expert"),
        P(None, "expert"),
    )

    def spread(body):
        return jax.shard_map(
            body, mesh=mesh, in_specs=specs, out_specs=P(("dp", "expert"), None), check_vma=False
        )

    if devices != 4 or mesh.shape["dp"] % 4:
        return spread(general_body)
    return spread(pair_body)
```

```python
import functools

import jax
import jax.numpy as jnp
from jax import lax
from jax.experimental import pallas as pl
from jax.experimental.pallas import tpu as pltpu
from jax.sharding import PartitionSpec as P

VMEM = pl.BlockSpec(memory_space=pltpu.VMEM)
ANY = pl.BlockSpec(memory_space=pl.ANY)
SLAB = 128
CUTS = (0, 5, 12, 16)


def general_body(expert_ids, gate_weights, hidden, hot_down, cold_down):
    devices = lax.axis_size("expert")
    group_size = min(4, devices)
    cold_count = devices // group_size
    experts_all = cold_count + 1
    tok_rows, top_count, hidden_width = hidden.shape
    capacity = 3 * tok_rows // 4 + tok_rows // 4 * (3 - min(experts_all, 3))
    flat_rows = tok_rows * top_count
    flat_hidden = hidden.reshape(flat_rows, hidden_width)
    flat_ids = expert_ids.reshape(flat_rows)
    hot_chosen = expert_ids == cold_count
    hot_rows = jnp.sum(
        jnp.where(hot_chosen[:, :, None], hidden, jnp.zeros((), hidden.dtype)), axis=1
    )
    hot_gate = jnp.sum(jnp.where(hot_chosen, gate_weights, jnp.zeros((), jnp.float32)), axis=1)
    hot_out = jnp.dot(
        hot_rows,
        lax.all_gather(hot_down, "expert", axis=1, tiled=True),
        preferred_element_type=jnp.float32,
    )
    hot_term = hot_gate[:, None] * hot_out
    onehot_expert = (flat_ids[None, :] == jnp.arange(cold_count, dtype=jnp.int32)[:, None]).astype(
        jnp.int32
    )
    slot_ranks = jnp.sum(onehot_expert * (jnp.cumsum(onehot_expert, axis=1) - 1), axis=0)
    slot_index = jnp.where(flat_ids < cold_count, flat_ids * capacity + slot_ranks, -1)
    placing = (
        jnp.arange(cold_count * capacity, dtype=jnp.int32)[:, None] == slot_index[None, :]
    ).astype(jnp.bfloat16)
    send_rows = jnp.dot(placing, flat_hidden, preferred_element_type=jnp.float32).astype(
        jnp.bfloat16
    )
    copies = jnp.broadcast_to(
        send_rows.reshape(cold_count, 1, capacity, hidden_width),
        (cold_count, group_size, capacity, hidden_width),
    ).reshape(devices, capacity, hidden_width)
    outputs = jnp.einsum(
        "nsf,fd->nsd",
        lax.all_to_all(copies, "expert", split_axis=0, concat_axis=0, tiled=True),
        cold_down,
        preferred_element_type=jnp.float32,
    ).astype(jnp.bfloat16)
    returned = lax.all_to_all(outputs, "expert", split_axis=0, concat_axis=0, tiled=True)
    column_blocks = returned.reshape(cold_count, group_size, capacity, -1)
    placing_blocks = placing.reshape(cold_count, capacity, flat_rows)
    row_outputs = jnp.einsum(
        "ecr,egcd->rgd", placing_blocks, column_blocks, preferred_element_type=jnp.float32
    )
    row_outputs = row_outputs.reshape(tok_rows, top_count, -1)
    scaled = row_outputs * gate_weights[:, :, None]
    cold_term = jnp.sum(scaled, axis=1)
    return (cold_term + hot_term).astype(jnp.bfloat16)


def near_core(*arrays):
    return [pltpu.with_memory_space_constraint(a, pltpu.VMEM) for a in arrays]


def in_hbm(*arrays):
    return [pltpu.with_memory_space_constraint(a, pltpu.HBM) for a in arrays]


def limit(mib):
    return pltpu.CompilerParams(vmem_limit_bytes=mib << 20)


def rows_of(hidden_ref, start, rows_ref, sem):
    flat = hidden_ref.reshape(hidden_ref.shape[0] * hidden_ref.shape[1], hidden_ref.shape[2])
    return pltpu.make_async_copy(flat.at[pl.ds(start, rows_ref.shape[0])], rows_ref, sem)


def take_kernel(hidden_ref, ids_ref, weights_ref, *refs):
    *row_refs, gates_ref, ids, weights, sems = refs
    small = [
        pltpu.make_async_copy(ids_ref, ids, sems.at[0]),
        pltpu.make_async_copy(weights_ref, weights, sems.at[1]),
    ]
    large, at = [], 0
    for i, rows_ref in enumerate(row_refs):
        large.append(rows_of(hidden_ref, at, rows_ref, sems.at[2 + i]))
        at += rows_ref.shape[0]
    for copy in small + large:
        copy.start()
    for copy in small:
        copy.wait()
    for e in range(2):
        gates_ref[2 * e : 2 * e + 2, :] = jnp.where(ids[...] == e, weights[...], 0.0)
    for copy in large:
        copy.wait()


def take(hidden, ids, weights, spans):
    tokens, choices, depth = hidden.shape
    shapes = [pltpu.VMEM(((b - a) * choices, depth), hidden.dtype) for a, b in spans]
    shapes.append(pltpu.VMEM((2 * choices, tokens), weights.dtype))
    *rows, gates = pl.pallas_call(
        take_kernel,
        name="take",
        out_shape=shapes,
        in_specs=[ANY] * 3,
        out_specs=[VMEM] * len(shapes),
        scratch_shapes=[
            pltpu.VMEM(ids.shape, ids.dtype),
            pltpu.VMEM(weights.shape, weights.dtype),
            pltpu.SemaphoreType.DMA((2 + len(spans),)),
        ],
        compiler_params=limit(2),
        cost_estimate=pl.CostEstimate(flops=0, bytes_accessed=4 * tokens * choices * depth, transcendentals=0),
    )(*in_hbm(hidden, ids, weights))
    return rows, gates


def choose(rows, gates):
    tokens = gates.shape[0]
    first = 2 * lax.broadcasted_iota(jnp.int32, (tokens, 2 * tokens), 0)
    column = lax.broadcasted_iota(jnp.int32, (tokens, 2 * tokens), 1)
    chosen, scales = [], []
    for expert in range(2):
        low, high = gates[:, 2 * expert : 2 * expert + 1], gates[:, 2 * expert + 1 : 2 * expert + 2]
        pick = (column == first + jnp.where(high != 0, 1, 0)).astype(rows.dtype)
        picked = jnp.dot(pick, rows, preferred_element_type=jnp.float32)
        chosen.append(picked.astype(rows.dtype))
        scales.append(low + high)
    return chosen, scales


def columns_of(gates_ref):
    return jnp.transpose(jnp.concatenate([gates_ref[...]] * 2, axis=0))


def gated(chosen, scales, weights):
    width = weights[0].shape[1]
    for at in range(0, width, SLAB):
        end = min(at + SLAB, width)
        terms = [
            scale * jnp.dot(x, w[:, at:end], preferred_element_type=jnp.float32)
            for scale, x, w in zip(scales, chosen, weights)
        ]
        yield at, end, terms[0] + terms[1]


def far_kernel(start, part_ref, whole_ref, gates_ref, c0, h0, c1, h1, out_ref, rows):
    tokens, width = out_ref.shape[0], c0.shape[1]
    core = lax.axis_index("expert") % 2

    @pl.when(core == 0)
    def _():
        rows[...] = part_ref[...]

    @pl.when(core == 1)
    def _():
        rows[...] = whole_ref[start : start + tokens].reshape(rows.shape)

    chosen, scales = choose(rows[...], columns_of(gates_ref)[start : start + tokens, :])
    for i, weights in enumerate(((c0, h0), (c1, h1))):
        for at, end, block in gated(chosen, scales, weights):
            out_ref[:, i * width + at : i * width + end] = block.astype(out_ref.dtype)


def cost_of(rows, width):
    return pl.CostEstimate(
        flops=4 * rows.shape[0] * rows.shape[1] * width, bytes_accessed=8 * rows.shape[0] * width, transcendentals=0
    )


def far_project(start, tokens, part, whole, gates, own, partner):
    width = own[0].shape[1]
    operands = [part, whole, gates, *own, *partner]
    return pl.pallas_call(
        functools.partial(far_kernel, start),
        name="far_project",
        out_shape=pltpu.VMEM((tokens, 2 * width), part.dtype),
        in_specs=[VMEM] * len(operands),
        out_specs=VMEM,
        scratch_shapes=[pltpu.VMEM(part.shape, part.dtype)],
        compiler_params=limit(12),
        cost_estimate=cost_of(part, width),
    )(*near_core(*operands))


def own_kernel(blocks, count, *refs):
    row_refs, rest = refs[:count], refs[count:]
    gates_ref, *weight_refs, whole_ref, out_ref, staged, sems = rest
    del whole_ref
    width = weight_refs[0].shape[1]
    me = lax.axis_index("expert")

    def write(names):
        gates = columns_of(gates_ref)
        chosen, scales, at = [], [], 0
        for rows_ref in row_refs:
            tokens = rows_ref.shape[0] // 2
            x, g = choose(rows_ref[...], gates[at : at + tokens, :])
            chosen.append(x)
            scales.append(g)
            at += tokens
        joined = [jnp.concatenate(x, axis=0) for x in zip(*chosen)]
        spread = [jnp.concatenate(g, axis=0) for g in zip(*scales)]
        copies = []
        for name in names:
            slot = [b for b, _ in blocks].index(name)
            for at, end, block in gated(joined, spread, weight_refs[2 * slot : 2 * slot + 2]):
                staged[name, :, at:end] = block.astype(staged.dtype)
            to = pl.multiple_of((me ^ name) * width, width)
            copies.append(pltpu.make_async_copy(staged.at[name], out_ref.at[:, pl.ds(to, width)], sems.at[name]))
            copies[-1].start()
        for copy in copies:
            copy.wait()

    if all(len(turns) == 2 for _, turns in blocks):
        write([name for name, _ in blocks])
        return
    for turn in range(2):
        names = [name for name, turns in blocks if turn in turns]
        if names:
            pl.when(me % 2 == turn)(functools.partial(write, names))


def own_project(blocks, rows, gates, weights, out):
    width = weights[0].shape[1]
    tokens = sum(r.shape[0] for r in rows) // 2
    operands = [*rows, gates, *weights]
    return pl.pallas_call(
        functools.partial(own_kernel, blocks, len(rows)),
        name="own_project",
        out_shape=pltpu.HBM(out.shape, out.dtype),
        in_specs=[VMEM] * len(operands) + [ANY],
        out_specs=ANY,
        scratch_shapes=[pltpu.VMEM((2, tokens, width), rows[0].dtype), pltpu.SemaphoreType.DMA((2,))],
        input_output_aliases={len(operands): 0},
        compiler_params=limit(12),
        cost_estimate=cost_of(rows[0], len(rows) * width * len(weights) // 4),
    )(*near_core(*operands), *in_hbm(out))


def fresh_kernel(out_ref):
    del out_ref


def fresh(shape, dtype):
    return pl.pallas_call(
        fresh_kernel,
        name="fresh",
        out_shape=pltpu.HBM(shape, dtype),
        out_specs=ANY,
        compiler_params=limit(2),
        cost_estimate=pl.CostEstimate(flops=0, bytes_accessed=0, transcendentals=0),
    )()


def put_kernel(starts, *refs):
    block_refs, (_, out_ref, sems) = refs[: len(starts)], refs[len(starts) :]
    me = lax.axis_index("expert")
    copies = []
    for start, block_ref in zip(starts, block_refs):
        tokens, width = block_ref.shape[0], block_ref.shape[1] // 2
        for i in range(2):
            to = pl.multiple_of((me ^ 2 ^ i) * width, width)
            copies.append(
                pltpu.make_async_copy(
                    block_ref.at[:, pl.ds(i * width, width)],
                    out_ref.at[pl.ds(start, tokens), pl.ds(to, width)],
                    sems.at[len(copies)],
                )
            )
            copies[-1].start()
    for copy in copies:
        copy.wait()


def put(starts, blocks, whole):
    count = len(starts)
    return pl.pallas_call(
        functools.partial(put_kernel, starts),
        name="put",
        out_shape=pltpu.HBM(whole.shape, whole.dtype),
        in_specs=[VMEM] * count + [ANY],
        out_specs=ANY,
        scratch_shapes=[pltpu.SemaphoreType.DMA((2 * count,))],
        input_output_aliases={count: 0},
        compiler_params=limit(2),
        cost_estimate=pl.CostEstimate(
            flops=0, bytes_accessed=4 * sum(b.size for b in blocks), transcendentals=0
        ),
    )(*near_core(*blocks), *in_hbm(whole))


def hold_kernel(*refs):
    ins, outs, sems = refs[: (len(refs) - 1) // 2], refs[(len(refs) - 1) // 2 : -1], refs[-1]
    copies = [pltpu.make_async_copy(a, b, sems.at[i]) for i, (a, b) in enumerate(zip(ins, outs))]
    for copy in copies:
        copy.start()
    for copy in copies:
        copy.wait()


def hold(*arrays):
    return pl.pallas_call(
        hold_kernel,
        name="hold",
        out_shape=[pltpu.VMEM(a.shape, a.dtype) for a in arrays],
        in_specs=[ANY] * len(arrays),
        out_specs=[VMEM] * len(arrays),
        scratch_shapes=[pltpu.SemaphoreType.DMA((len(arrays),))],
        compiler_params=limit(2),
        cost_estimate=pl.CostEstimate(
            flops=0, bytes_accessed=4 * sum(a.size for a in arrays), transcendentals=0
        ),
    )(*in_hbm(*arrays))


def pair_body(expert_ids, gate_weights, hidden, hot_down, cold_down):
    devices, groups = lax.axis_size("expert"), lax.axis_size("dp")
    near = [(i, i ^ 1) for i in range(devices)]
    far = [(i, i ^ 2) for i in range(devices)]
    tokens = hidden.shape[0]
    cuts = [tokens * c // 16 for c in CUTS]
    spans = list(zip(cuts[:-1], cuts[1:]))

    def send(array, pairs):
        return lax.ppermute(array, "expert", pairs)

    def send_by(array, core):
        pairs = [
            (g * devices + i, g * devices + (i ^ 2) if i % 2 == core else (g ^ (2 - core)) * devices + i)
            for g in range(groups)
            for i in range(devices)
        ]
        return lax.ppermute(array, ("dp", "expert"), pairs)

    whole = send_by(hidden, 1)
    held, gates = take(hidden, expert_ids.T, gate_weights.T, spans)
    moved = [send_by(rows, 0) for rows in held]
    far_gates = send(gates, far)
    partner = (send(cold_down, near), send(hot_down, near))
    out = fresh((tokens, devices * hot_down.shape[1]), hidden.dtype)
    own = hold(cold_down, hot_down)
    back = []
    for i, (a, b) in enumerate(spans):
        if i == 2:
            out = own_project(((0, (1,)), (1, (1,))), held, gates, (*own, *partner), out)
        result = far_project(a, b - a, moved[i], whole, far_gates, own, partner)
        back.append(send(result, far))
    out = own_project(((0, (0,)), (1, (0,))), held, gates, (*own, *partner), out)
    starts = [a for a, _ in spans]
    out = put(starts[:-1], back[:-1], out)
    out = put(starts[-1:], back[-1:], out)
    return out


def solution(mesh):
    devices = mesh.shape["expert"]
    specs = (
        P(("dp", "expert"), None),
        P(("dp", "expert"), None),
        P(("dp", "expert"), None, None),
        P(None, "expert"),
        P(None, "expert"),
    )

    def spread(body):
        return jax.shard_map(
            body, mesh=mesh, in_specs=specs, out_specs=P(("dp", "expert"), None), check_vma=False
        )

    if devices != 4 or mesh.shape["dp"] % 4:
        return spread(general_body)
    return spread(pair_body)
```
